256 devices in a mesh: band: 8 (over x, y_lo), space: 32 (over z, y_hi, core).
Axes of the slice: x: 4, y: 4 (y_hi: 2, y_lo: 2; y = y_hi * 2 + y_lo), z: 8, core: 2. Of those that a mesh axis runs over, the one named last changes fastest.
Arguments:
- orbitals: float32 [8, 192, 192, 192], P('band', 'space'), may hold values from -6 to 6
- occupations: int32 [8], replicated, may hold values from 1 to 4
Outputs:
- exchange_potential: float32 [8, 192, 192, 192], P('band', 'space')
The draws below stay inside these ranges and needn't reach their ends.
All inputs are finite; a program needn't handle non-finite values.
Results may differ from the reference program's by a relative error of at most 0.0003.
Values sent between devices are 32-bit elements; how exact they have to be, the bound alone decides.
No kernel may reach another device: no remote copies, remote signals or barrier semaphores. Data moves between devices by JAX's collectives and lax.ppermute only.
A program may use at most 64 MiB of HBM per device.

```python
import math
import jax
import jax.numpy as jnp
import numpy as np
from jax import lax

GRID = 192
BAND_DEV = 1
STEPS = 2
GROUPS = 8
BANDS = 8


def draw_orbitals(key, part):
    shape = (BANDS, GRID, GRID, GRID)
    return jnp.clip(jax.random.normal(key, shape, jnp.float32), -6.0, 6.0)


def plant(entries, own_key, smallest, high):
    shape = entries.shape
    place = [jax.random.randint(jax.random.fold_in(own_key, axis), (), 0, shape[axis]) for axis in range(len(shape))]
    entries = entries.at[tuple(place)].set(smallest)
    longest = shape.index(max(shape))
    place[longest] = (place[longest] + 1) % shape[longest]
    return entries.at[tuple(place)].set(high)


def setup_inputs(seed: int = 0) -> dict:
    key_list = jax.random.split(jax.random.key(seed), 3)
    orbitals = draw_orbitals(jax.random.fold_in(key_list[2], 71), 0)
    occupations = plant(jax.random.randint(key_list[1], (BANDS,), 1, 5), jax.random.fold_in(key_list[1], 1), 1, 4).astype(jnp.int32)
    return dict(orbitals=orbitals, occupations=occupations)


def screened_kernel():
    indices = jnp.arange(GRID, dtype=jnp.int32)
    folded = jnp.minimum(indices, GRID - indices)
    half_line = folded[: GRID // 2 + 1]
    squares = folded[:, None, None] ** 2 + folded[None, :, None] ** 2 + half_line[None, None, :] ** 2
    lowest = (2.0 * math.pi / GRID) ** 2
    values = 1.0 / (lowest * (1.0 + squares.astype(jnp.float32)))
    return jnp.where(squares > 0, values, jnp.zeros_like(values))


def pair_table():
    left_list, right_list, repeat_list = [], [], []
    for left_band in range(BANDS):
        for right_band in range(left_band, BANDS):
            offset = right_band // BAND_DEV - left_band // BAND_DEV
            repeats = sum(1 for shift in range(-STEPS, STEPS + 1) if (offset - shift) % GROUPS == 0)
            if repeats > 0:
                left_list.append(left_band)
                right_list.append(right_band)
                repeat_list.append(repeats)
    return (np.array(left_list, dtype=np.int32), np.array(right_list, dtype=np.int32),
            np.array(repeat_list, dtype=np.int32))


def reference(orbitals, occupations):
    kernel = screened_kernel()
    weights = occupations.astype(jnp.float32)
    left_arr, right_arr, repeat_arr = pair_table()

    def accumulate(total, item):
        left_band, right_band, repeats = item
        phi_left = lax.dynamic_index_in_dim(orbitals, left_band, 0, keepdims=False)
        phi_right = lax.dynamic_index_in_dim(orbitals, right_band, 0, keepdims=False)
        density = phi_left * phi_right
        spectrum = jnp.fft.rfftn(density)
        field = jnp.fft.irfftn(spectrum * kernel, s=(GRID, GRID, GRID)).astype(orbitals.dtype)
        scale = repeats.astype(orbitals.dtype)
        total = total.at[left_band].add(scale * weights[right_band] * phi_right * field)
        other = jnp.where(left_band != right_band, scale * weights[left_band], jnp.zeros_like(scale))
        total = total.at[right_band].add(other * phi_left * field)
        return total, None

    start = jnp.zeros(orbitals.shape, dtype=orbitals.dtype)
    total, _ = lax.scan(accumulate, start, (jnp.asarray(left_arr), jnp.asarray(right_arr), jnp.asarray(repeat_arr)))
    return -total
```

```python
import math

import jax
import jax.numpy as jnp
import ml_dtypes
import numpy as np
from jax import lax
from jax.experimental import pallas as pl
from jax.experimental.pallas import tpu as pltpu
from jax.sharding import PartitionSpec as P

LANES = 128
HALF = 64
SLOTS = 8
VMEM = pl.BlockSpec(memory_space=pltpu.VMEM)
SMEM = pl.BlockSpec(memory_space=pltpu.SMEM)


def tables(length, slabs, rows):
    index = np.arange(length)
    phase = (index[:, None] * index[None, :]) % length * (2.0 * math.pi / length)
    cas = np.cos(phase) + np.sin(phase)
    wide = np.concatenate([np.arange(LANES), np.arange(LANES, length), np.arange(LANES, length)])
    grouped = np.array([rows * slab + row for row in range(rows) for slab in range(slabs)])
    padded = np.zeros((length, slabs, SLOTS))
    padded[:, :, :rows] = cas.reshape(length, slabs, rows)
    padded = padded.reshape(length, slabs * SLOTS)
    parts = {
        "z": cas[:, wide],
        "y": cas[grouped, :],
        "x": padded,
        "xt": padded.T,
        "yt": cas[:, grouped],
        "zt": cas[wide, :],
    }
    places, pieces, start = {}, [], 0
    for name, part in parts.items():
        height, width = part.shape
        places[name] = (start, height, width)
        start += 2 * height
        high = part.astype(ml_dtypes.bfloat16)
        low = (part - high.astype(np.float64)).astype(ml_dtypes.bfloat16)
        both = np.zeros((2 * height, 2 * LANES), ml_dtypes.bfloat16)
        both[:height, :width], both[height:, :width] = high, low
        pieces.append(both)
    return places, jnp.asarray(np.concatenate(pieces))


def terms(table_ref, place):
    start, height, width = place
    return table_ref[start : start + height, :width], table_ref[start + height : start + 2 * height, :width]


def split(value):
    high = value.astype(jnp.bfloat16)
    return high, (value - high.astype(jnp.float32)).astype(jnp.bfloat16)


def product(left, right):
    def dot(a, b):
        return jnp.dot(a, b, preferred_element_type=jnp.float32)

    return dot(left[0], right[0]) + (dot(left[0], right[1]) + dot(left[1], right[0]))


def call(kernel, out_shape, flops, size, in_specs, scratch=()):
    return pl.pallas_call(
        kernel,
        out_shape=out_shape,
        in_specs=in_specs,
        out_specs=jax.tree.map(lambda _: VMEM, out_shape),
        scratch_shapes=list(scratch),
        compiler_params=pltpu.CompilerParams(vmem_limit_bytes=16 * 1024 * 1024),
        cost_estimate=pl.CostEstimate(flops=flops, bytes_accessed=size, transcendentals=0),
    )


def lower_lanes():
    return lax.broadcasted_iota(jnp.int32, (1, LANES), 1) < HALF


def pack(value):
    half = value.shape[0] // 2
    rest = jnp.concatenate([value[:half, LANES:], value[half:, LANES:]], axis=1)
    return jnp.concatenate([value[:, :LANES], rest], axis=0)


def unpack(packed, length):
    rest = packed[length:]
    column = jnp.concatenate([rest[:, :HALF], rest[:, HALF:]], axis=0)
    return jnp.concatenate([packed[:length], column], axis=1)


def packed_shape(rows, length):
    return jax.ShapeDtypeStruct((rows, length * length // LANES, LANES), jnp.float32)


def packed_planes(orbitals):
    rows, length, _ = orbitals.shape

    def kernel(planes, out):
        for plane in range(rows):
            out[plane] = pack(planes[plane])

    return call(kernel, packed_shape(rows, length), 2**18, 2**21, [VMEM])(orbitals)


def forward(own, guests, table):
    places, entries, rows, length = table
    slabs = length // rows
    count = len(guests)
    block = rows * rows * length // LANES
    points = length * length

    def kernel(*refs):
        own_ref, guest_refs, table_ref, out = refs[0], refs[1 : 1 + count], refs[1 + count], refs[-1]
        z_table, y_table = terms(table_ref, places["z"]), terms(table_ref, places["y"])
        lower = lower_lanes()
        corner = (lax.broadcasted_iota(jnp.int32, (slabs, LANES), 0) == 0) & (
            lax.broadcasted_iota(jnp.int32, (slabs, LANES), 1) == 0
        )
        for number, guest in enumerate(guest_refs):
            for plane in range(rows):
                density = own_ref[plane] * guest[plane]
                mean = jnp.sum(density, keepdims=True) * (1.0 / points)
                along = product(split(unpack(density - mean, length)), z_table)
                both = product(y_table, split(along))
                base = number * block + plane
                for row in range(rows):
                    piece = both[slabs * row : slabs * (row + 1), :LANES]
                    if row == 0:
                        piece = piece + jnp.where(corner, mean * float(points), 0.0)
                    out[:, base + rows * row, :] = piece
                for row in range(0, rows, 2):
                    even = both[slabs * row : slabs * (row + 1), LANES:]
                    odd = both[slabs * (row + 1) : slabs * (row + 2), LANES:]
                    out[:, base + rows * (rows + row // 2), :] = jnp.where(lower, even, odd)

    shape = jax.ShapeDtypeStruct((slabs, count * block, LANES), jnp.float32)
    work = call(kernel, shape, count * 12 * length**3 * rows, count * 2**22, [VMEM] * (2 + count))
    return work(own, *guests, entries)


def middle(blocks, pairs, kernel_values, table):
    places, entries, rows, length = table
    slabs = length // rows
    width = kernel_values.shape[1]
    groups = width // LANES
    depth = groups * rows
    tile = 2 * LANES
    lanes = len(pairs) * width

    def kernel(in_ref, values, table_ref, out, lines):
        lines[:, rows:, :] = jnp.zeros((slabs, SLOTS - rows, lanes), jnp.float32)
        for group in range(len(pairs) * groups):
            base = pairs[group // groups] * depth + rows * (group % groups)
            lines[:, :rows, LANES * group : LANES * (group + 1)] = in_ref[:, base : base + rows, :]
        x_table, back_table = terms(table_ref, places["x"]), terms(table_ref, places["xt"])
        for start in range(0, lanes, tile):
            stop = min(start + tile, lanes)
            line = lines[:, :, start:stop].reshape(slabs * SLOTS, stop - start)
            total = jnp.sum(line, axis=0, keepdims=True)
            spectrum = product(x_table, split(line - total * (1.0 / length)))
            first_row = lax.broadcasted_iota(jnp.int32, spectrum.shape, 0) == 0
            spectrum = spectrum + jnp.where(first_row, total, 0.0)
            scaled = [
                spectrum[:, first - start : first - start + LANES] * values[:, first % width : first % width + LANES]
                for first in range(start, stop, LANES)
            ]
            image = jnp.concatenate(scaled, axis=1)
            solved = product(back_table, split(image)).reshape(slabs, SLOTS, stop - start)
            for first in range(start, stop, LANES):
                place = rows * (first // LANES)
                out[:, place : place + rows, :] = solved[:, :rows, first - start : first - start + LANES]

    shape = jax.ShapeDtypeStruct((slabs, len(pairs) * depth, LANES), jnp.float32)
    scratch = [pltpu.VMEM((slabs, SLOTS, lanes), jnp.float32)]
    work = call(kernel, shape, lanes * 12 * length * length, lanes * 2**12, [VMEM] * 3, scratch)
    return work(blocks, kernel_values, entries)


def potential_plane(block_ref, place, rows, y_table, z_table, lower):
    full = jnp.concatenate([block_ref[:, place + rows * row, :] for row in range(rows)], axis=0)
    parts = []
    for row in range(rows // 2):
        shared = block_ref[:, place + rows * (rows + row), :]
        parts.append(jnp.where(lower, shared, 0.0))
        parts.append(jnp.where(lower, 0.0, shared))
    wide = jnp.concatenate([full, jnp.concatenate(parts, axis=0)], axis=1)
    along = product(y_table, split(wide))
    return pack(product(split(along), z_table))


def apply_pairs(blocks, own, guests, weights, table):
    places, entries, rows, length = table
    count = len(guests)
    block = rows * rows * length // LANES

    def kernel(weight, block_ref, own_ref, *refs):
        guest_refs, table_ref, total, sent = refs[:count], refs[count], refs[count + 1], refs[count + 2 :]
        lower = lower_lanes()
        y_table, z_table = terms(table_ref, places["yt"]), terms(table_ref, places["zt"])
        for number in range(count):
            for plane in range(rows):
                field = potential_plane(block_ref, number * block + plane, rows, y_table, z_table, lower)
                term = (weight[number + 1] * guest_refs[number][plane]) * field
                total[plane] = term if number == 0 else total[plane] + term
                sent[number][plane] = (weight[0] * own_ref[plane]) * field

    shape = packed_shape(rows, length)
    work = call(kernel, [shape] * (1 + count), count * 12 * length**3 * rows, count * 2**22, [SMEM] + [VMEM] * (3 + count))
    return work(weights, blocks, own, *guests, entries)


def apply_own(blocks, own, partial, weights, table):
    places, entries, rows, length = table

    def kernel(weight, block_ref, own_ref, part, table_ref, total):
        lower = lower_lanes()
        y_table, z_table = terms(table_ref, places["yt"]), terms(table_ref, places["zt"])
        for plane in range(rows):
            field = potential_plane(block_ref, plane, rows, y_table, z_table, lower)
            total[plane] = part[plane] + (weight[0] * own_ref[plane]) * field

    work = call(kernel, packed_shape(rows, length), 12 * length**3 * rows, 2**22, [SMEM] + [VMEM] * 4)
    return work(weights, blocks, own, partial, entries)


def finish(total, received, rows, length):
    def kernel(total_ref, first, second, out):
        for plane in range(rows):
            out[plane] = -unpack(total_ref[plane] + (first[plane] + second[plane]), length)

    shape = jax.ShapeDtypeStruct((rows, length, length), jnp.float32)
    return call(kernel, shape, 2**20, 2**22, [VMEM] * 3)(total, *received)


def kernel_lines(length, rows, slab):
    width = rows * length
    shape = (length, width)
    column = lax.broadcasted_iota(jnp.int32, shape, 1)
    group, lane = column // LANES, column % LANES
    shared = group >= rows
    row = jnp.where(shared, 2 * (group - rows) + lane // HALF, group)
    third = jnp.where(shared, LANES + lane % HALF, lane)

    def square(index):
        folded = jnp.minimum(index, length - index)
        return folded * folded

    total = square(lax.broadcasted_iota(jnp.int32, shape, 0)) + square(slab * rows + row) + square(third)
    lowest = (2.0 * math.pi / length) ** 2
    values = 1.0 / (lowest * (1.0 + total.astype(jnp.float32)))
    return jnp.where(total > 0, values, jnp.zeros_like(values)) / float(length**3)


def exchange(blocks):
    return lax.all_to_all(blocks, "space", split_axis=0, concat_axis=0, tiled=True)


def shards(orbitals, occupations):
    rows, length = orbitals.shape[1:3]
    slabs = lax.axis_size("space")
    groups = lax.axis_size("band")
    band = lax.axis_index("band")
    table = tables(length, slabs, rows) + (rows, length)

    def shifted(array, by):
        return lax.ppermute(array, "band", [(group, (group + by) % groups) for group in range(groups)])

    own = packed_planes(orbitals[0])
    guests = [shifted(own, -1), shifted(own, 2)]
    picks = jnp.stack([band, (band + 1) % groups, (band + groups - 2) % groups])
    weights = occupations.astype(jnp.float32)[picks]
    kernel_values = kernel_lines(length, rows, lax.axis_index("space"))

    lines = exchange(forward(own, guests + [own], table))
    pair_back = exchange(middle(lines, [0, 1], kernel_values, table))
    own_image = middle(lines, [2], kernel_values, table)
    partial, to_next, to_far = apply_pairs(pair_back, own, guests, weights, table)
    received = [shifted(to_next, 1), shifted(to_far, -2)]
    own_image, partial = lax.optimization_barrier((own_image, partial))
    own_back = exchange(own_image)
    total = apply_own(own_back, own, partial, weights, table)
    return finish(total, received, rows, length)[None]


def solution(mesh):
    placed = (P("band", "space", None, None), P())
    return jax.shard_map(
        shards,
        mesh=mesh,
        in_specs=placed,
        out_specs=P("band", "space", None, None),
        check_vma=False,
    )
```

```python
import math

import jax
import jax.numpy as jnp
import ml_dtypes
import numpy as np
from jax import lax
from jax.experimental import pallas as pl
from jax.experimental.pallas import tpu as pltpu
from jax.sharding import PartitionSpec as P

LANES = 128
HALF = 64
SLOTS = 8
VMEM = pl.BlockSpec(memory_space=pltpu.VMEM)
SMEM = pl.BlockSpec(memory_space=pltpu.SMEM)


def tables(length, slabs, rows):
    index = np.arange(length)
    phase = (index[:, None] * index[None, :]) % length * (2.0 * math.pi / length)
    cas = np.cos(phase) + np.sin(phase)
    wide = np.concatenate([np.arange(LANES), np.arange(LANES, length), np.arange(LANES, length)])
    grouped = np.array([rows * slab + row for row in range(rows) for slab in range(slabs)])
    padded = np.zeros((length, slabs, SLOTS))
    padded[:, :, :rows] = cas.reshape(length, slabs, rows)
    padded = padded.reshape(length, slabs * SLOTS)
    parts = {
        "z": cas[:, wide],
        "y": cas[grouped, :],
        "x": padded,
        "xt": padded.T,
        "yt": cas[:, grouped],
        "zt": cas[wide, :],
    }
    places, pieces, start = {}, [], 0
    for name, part in parts.items():
        height, width = part.shape
        places[name] = (start, height, width)
        start += 2 * height
        high = part.astype(ml_dtypes.bfloat16)
        low = (part - high.astype(np.float64)).astype(ml_dtypes.bfloat16)
        both = np.zeros((2 * height, 2 * LANES), ml_dtypes.bfloat16)
        both[:height, :width], both[height:, :width] = high, low
        pieces.append(both)
    return places, jnp.asarray(np.concatenate(pieces))


def terms(table_ref, place):
    start, height, width = place
    return table_ref[start : start + height, :width], table_ref[start + height : start + 2 * height, :width]


def split(value):
    high = value.astype(jnp.bfloat16)
    return high, (value - high.astype(jnp.float32)).astype(jnp.bfloat16)


def product(left, right):
    def dot(a, b):
        return jnp.dot(a, b, preferred_element_type=jnp.float32)

    return dot(left[0], right[0]) + (dot(left[0], right[1]) + dot(left[1], right[0]))


def call(kernel, out_shape, flops, size, in_specs, scratch=()):
    return pl.pallas_call(
        kernel,
        out_shape=out_shape,
        in_specs=in_specs,
        out_specs=jax.tree.map(lambda _: VMEM, out_shape),
        scratch_shapes=list(scratch),
        compiler_params=pltpu.CompilerParams(vmem_limit_bytes=16 * 1024 * 1024),
        cost_estimate=pl.CostEstimate(flops=flops, bytes_accessed=size, transcendentals=0),
    )


def lower_lanes():
    return lax.broadcasted_iota(jnp.int32, (1, LANES), 1) < HALF


def pack(value):
    half = value.shape[0] // 2
    rest = jnp.concatenate([value[:half, LANES:], value[half:, LANES:]], axis=1)
    return jnp.concatenate([value[:, :LANES], rest], axis=0)


def unpack(packed, length):
    rest = packed[length:]
    column = jnp.concatenate([rest[:, :HALF], rest[:, HALF:]], axis=0)
    return jnp.concatenate([packed[:length], column], axis=1)


def packed_shape(rows, length):
    return jax.ShapeDtypeStruct((rows, length * length // LANES, LANES), jnp.float32)


def packed_planes(orbitals):
    rows, length, _ = orbitals.shape

    def kernel(planes, out):
        for plane in range(rows):
            out[plane] = pack(planes[plane])

    return call(kernel, packed_shape(rows, length), 2**18, 2**21, [VMEM])(orbitals)


def forward(own, guests, table, weight=1):
    places, entries, rows, length = table
    slabs = length // rows
    count = len(guests)
    block = rows * rows * length // LANES
    points = length * length

    def kernel(*refs):
        own_ref, guest_refs, table_ref, out = refs[0], refs[1 : 1 + count], refs[1 + count], refs[-1]
        z_table, y_table = terms(table_ref, places["z"]), terms(table_ref, places["y"])
        lower = lower_lanes()
        corner = (lax.broadcasted_iota(jnp.int32, (slabs, LANES), 0) == 0) & (
            lax.broadcasted_iota(jnp.int32, (slabs, LANES), 1) == 0
        )
        for number, guest in enumerate(guest_refs):
            for plane in range(rows):
                density = own_ref[plane] * guest[plane]
                mean = jnp.sum(density, keepdims=True) * (1.0 / points)
                along = product(split(unpack(density - mean, length)), z_table)
                both = product(y_table, split(along))
                base = number * block + plane
                for row in range(rows):
                    piece = both[slabs * row : slabs * (row + 1), :LANES]
                    if row == 0:
                        piece = piece + jnp.where(corner, mean * float(points), 0.0)
                    out[:, base + rows * row, :] = piece
                for row in range(0, rows, 2):
                    even = both[slabs * row : slabs * (row + 1), LANES:]
                    odd = both[slabs * (row + 1) : slabs * (row + 2), LANES:]
                    out[:, base + rows * (rows + row // 2), :] = jnp.where(lower, even, odd)

    shape = jax.ShapeDtypeStruct((slabs, count * block, LANES), jnp.float32)
    work = call(kernel, shape, weight * count * 12 * length**3 * rows, count * 2**22, [VMEM] * (2 + count))
    return work(own, *guests, entries)


def middle(blocks, pairs, kernel_values, table):
    places, entries, rows, length = table
    slabs = length // rows
    width = kernel_values.shape[1]
    groups = width // LANES
    depth = groups * rows
    tile = 2 * LANES
    lanes = len(pairs) * width

    def kernel(in_ref, values, table_ref, out, lines):
        lines[:, rows:, :] = jnp.zeros((slabs, SLOTS - rows, lanes), jnp.float32)
        for group in range(len(pairs) * groups):
            base = pairs[group // groups] * depth + rows * (group % groups)
            lines[:, :rows, LANES * group : LANES * (group + 1)] = in_ref[:, base : base + rows, :]
        x_table, back_table = terms(table_ref, places["x"]), terms(table_ref, places["xt"])
        for start in range(0, lanes, tile):
            stop = min(start + tile, lanes)
            line = lines[:, :, start:stop].reshape(slabs * SLOTS, stop - start)
            total = jnp.sum(line, axis=0, keepdims=True)
            spectrum = product(x_table, split(line - total * (1.0 / length)))
            first_row = lax.broadcasted_iota(jnp.int32, spectrum.shape, 0) == 0
            spectrum = spectrum + jnp.where(first_row, total, 0.0)
            scaled = [
                spectrum[:, first - start : first - start + LANES] * values[:, first % width : first % width + LANES]
                for first in range(start, stop, LANES)
            ]
            image = jnp.concatenate(scaled, axis=1)
            solved = product(back_table, split(image)).reshape(slabs, SLOTS, stop - start)
            for first in range(start, stop, LANES):
                place = rows * (first // LANES)
                out[:, place : place + rows, :] = solved[:, :rows, first - start : first - start + LANES]

    shape = jax.ShapeDtypeStruct((slabs, len(pairs) * depth, LANES), jnp.float32)
    scratch = [pltpu.VMEM((slabs, SLOTS, lanes), jnp.float32)]
    work = call(kernel, shape, lanes * 12 * length * length, lanes * 2**12, [VMEM] * 3, scratch)
    return work(blocks, kernel_values, entries)


def potential_plane(block_ref, place, rows, y_table, z_table, lower):
    full = jnp.concatenate([block_ref[:, place + rows * row, :] for row in range(rows)], axis=0)
    parts = []
    for row in range(rows // 2):
        shared = block_ref[:, place + rows * (rows + row), :]
        parts.append(jnp.where(lower, shared, 0.0))
        parts.append(jnp.where(lower, 0.0, shared))
    wide = jnp.concatenate([full, jnp.concatenate(parts, axis=0)], axis=1)
    along = product(y_table, split(wide))
    return pack(product(split(along), z_table))


def apply_pairs(blocks, own, guests, weights, table):
    places, entries, rows, length = table
    count = len(guests)
    block = rows * rows * length // LANES

    def kernel(weight, block_ref, own_ref, *refs):
        guest_refs, table_ref, total, sent = refs[:count], refs[count], refs[count + 1], refs[count + 2 :]
        lower = lower_lanes()
        y_table, z_table = terms(table_ref, places["yt"]), terms(table_ref, places["zt"])
        for number in range(count):
            for plane in range(rows):
                field = potential_plane(block_ref, number * block + plane, rows, y_table, z_table, lower)
                term = (weight[number + 1] * guest_refs[number][plane]) * field
                total[plane] = term if number == 0 else total[plane] + term
                sent[number][plane] = (weight[0] * own_ref[plane]) * field

    shape = packed_shape(rows, length)
    work = call(kernel, [shape] * (1 + count), count * 12 * length**3 * rows, count * 2**22, [SMEM] + [VMEM] * (3 + count))
    return work(weights, blocks, own, *guests, entries)


def add_received(partial, received):
    rows = partial.shape[0]

    def kernel(part, first, second, out):
        for plane in range(rows):
            out[plane] = part[plane] + (first[plane] + second[plane])

    shape = jax.ShapeDtypeStruct(partial.shape, jnp.float32)
    return call(kernel, shape, 2**34, 2**22, [VMEM] * 3)(partial, *received)


def apply_own(blocks, own, others, weights, table):
    places, entries, rows, length = table

    def kernel(weight, block_ref, own_ref, other, table_ref, out):
        lower = lower_lanes()
        y_table, z_table = terms(table_ref, places["yt"]), terms(table_ref, places["zt"])
        for plane in range(rows):
            field = potential_plane(block_ref, plane, rows, y_table, z_table, lower)
            out[plane] = -unpack(other[plane] + (weight[0] * own_ref[plane]) * field, length)

    shape = jax.ShapeDtypeStruct((rows, length, length), jnp.float32)
    work = call(kernel, shape, 12 * length**3 * rows, 2**22, [SMEM] + [VMEM] * 4)
    return work(weights, blocks, own, others, entries)


def kernel_lines(length, rows, slab):
    width = rows * length
    shape = (length, width)
    column = lax.broadcasted_iota(jnp.int32, shape, 1)
    group, lane = column // LANES, column % LANES
    shared = group >= rows
    row = jnp.where(shared, 2 * (group - rows) + lane // HALF, group)
    third = jnp.where(shared, LANES + lane % HALF, lane)

    def square(index):
        folded = jnp.minimum(index, length - index)
        return folded * folded

    total = square(lax.broadcasted_iota(jnp.int32, shape, 0)) + square(slab * rows + row) + square(third)
    lowest = (2.0 * math.pi / length) ** 2
    values = 1.0 / (lowest * (1.0 + total.astype(jnp.float32)))
    return jnp.where(total > 0, values, jnp.zeros_like(values)) / float(length**3)


def exchange(blocks):
    return lax.all_to_all(blocks, "space", split_axis=0, concat_axis=0, tiled=True)


def shards(orbitals, occupations):
    rows, length = orbitals.shape[1:3]
    slabs = lax.axis_size("space")
    groups = lax.axis_size("band")
    band = lax.axis_index("band")
    table = tables(length, slabs, rows) + (rows, length)

    def shifted(array, by):
        return lax.ppermute(array, "band", [(group, (group + by) % groups) for group in range(groups)])

    own = packed_planes(orbitals[0])
    guests = [shifted(own, -1), shifted(own, 2)]
    picks = jnp.stack([band, (band + 1) % groups, (band + groups - 2) % groups])
    weights = occupations.astype(jnp.float32)[picks]
    kernel_values = kernel_lines(length, rows, lax.axis_index("space"))

    own_lines = exchange(forward(own, [own], table))
    pair_blocks = forward(own, guests, table, 16)
    pair_blocks, own_lines = lax.optimization_barrier((pair_blocks, own_lines))
    pair_lines = exchange(pair_blocks)
    own_image = middle(own_lines, [0], kernel_values, table)
    pair_back = exchange(middle(pair_lines, [0, 1], kernel_values, table))
    own_image, pair_back = lax.optimization_barrier((own_image, pair_back))
    own_back = exchange(own_image)
    partial, to_next, to_far = apply_pairs(pair_back, own, guests, weights, table)
    received = [shifted(to_next, 1), shifted(to_far, -2)]
    others = add_received(partial, received)
    return apply_own(own_back, own, others, weights, table)[None]


def solution(mesh):
    placed = (P("band", "space", None, None), P())
    return jax.shard_map(
        shards,
        mesh=mesh,
        in_specs=placed,
        out_specs=P("band", "space", None, None),
        check_vma=False,
    )
```

```python
import math

import jax
import jax.numpy as jnp
import ml_dtypes
import numpy as np
from jax import lax
from jax.experimental import pallas as pl
from jax.experimental.pallas import tpu as pltpu
from jax.sharding import PartitionSpec as P

LANES = 128
HALF = 64
SLOTS = 8
VMEM = pl.BlockSpec(memory_space=pltpu.VMEM)
SMEM = pl.BlockSpec(memory_space=pltpu.SMEM)


def tables(length, slabs, rows):
    index = np.arange(length)
    phase = (index[:, None] * index[None, :]) % length * (2.0 * math.pi / length)
    cas = np.cos(phase) + np.sin(phase)
    wide = np.concatenate([np.arange(LANES), np.arange(LANES, length), np.arange(LANES, length)])
    grouped = np.array([rows * slab + row for row in range(rows) for slab in range(slabs)])
    padded = np.zeros((length, slabs, SLOTS))
    padded[:, :, :rows] = cas.reshape(length, slabs, rows)
    padded = padded.reshape(length, slabs * SLOTS)
    parts = {
        "z": cas[:, wide],
        "y": cas[grouped, :],
        "x": padded,
        "xt": padded.T,
        "yt": cas[:, grouped],
        "zt": cas[wide, :],
    }
    places, pieces, start = {}, [], 0
    for name, part in parts.items():
        height, width = part.shape
        places[name] = (start, height, width)
        start += 2 * height
        high = part.astype(ml_dtypes.bfloat16)
        low = (part - high.astype(np.float64)).astype(ml_dtypes.bfloat16)
        both = np.zeros((2 * height, 2 * LANES), ml_dtypes.bfloat16)
        both[:height, :width], both[height:, :width] = high, low
        pieces.append(both)
    return places, jnp.asarray(np.concatenate(pieces))


def terms(table_ref, place):
    start, height, width = place
    return table_ref[start : start + height, :width], table_ref[start + height : start + 2 * height, :width]


def split(value):
    high = value.astype(jnp.bfloat16)
    return high, (value - high.astype(jnp.float32)).astype(jnp.bfloat16)


def product(left, right):
    def dot(a, b):
        return jnp.dot(a, b, preferred_element_type=jnp.float32)

    return dot(left[0], right[0]) + (dot(left[0], right[1]) + dot(left[1], right[0]))


def call(kernel, out_shape, flops, size, in_specs, scratch=()):
    return pl.pallas_call(
        kernel,
        out_shape=out_shape,
        in_specs=in_specs,
        out_specs=jax.tree.map(lambda _: VMEM, out_shape),
        scratch_shapes=list(scratch),
        compiler_params=pltpu.CompilerParams(vmem_limit_bytes=16 * 1024 * 1024),
        cost_estimate=pl.CostEstimate(flops=flops, bytes_accessed=size, transcendentals=0),
    )


def lower_lanes():
    return lax.broadcasted_iota(jnp.int32, (1, LANES), 1) < HALF


def pack(value):
    half = value.shape[0] // 2
    rest = jnp.concatenate([value[:half, LANES:], value[half:, LANES:]], axis=1)
    return jnp.concatenate([value[:, :LANES], rest], axis=0)


def unpack(packed, length):
    rest = packed[length:]
    column = jnp.concatenate([rest[:, :HALF], rest[:, HALF:]], axis=0)
    return jnp.concatenate([packed[:length], column], axis=1)


def packed_shape(rows, length):
    return jax.ShapeDtypeStruct((rows, length * length // LANES, LANES), jnp.float32)


def packed_planes(orbitals):
    rows, length, _ = orbitals.shape

    def kernel(planes, out):
        for plane in range(rows):
            out[plane] = pack(planes[plane])

    return call(kernel, packed_shape(rows, length), 2**18, 2**21, [VMEM])(orbitals)


def block_pitch(depth):
    return depth


def forward(own, guests, table, weight=1):
    places, entries, rows, length = table
    slabs = length // rows
    count = len(guests)
    block = rows * rows * length // LANES
    pitch = block_pitch(count * block)
    points = length * length

    def kernel(*refs):
        own_ref, guest_refs, table_ref, out = refs[0], refs[1 : 1 + count], refs[1 + count], refs[-1]
        z_table, y_table = terms(table_ref, places["z"]), terms(table_ref, places["y"])
        lower = lower_lanes()
        corner = (lax.broadcasted_iota(jnp.int32, (slabs, LANES), 0) == 0) & (
            lax.broadcasted_iota(jnp.int32, (slabs, LANES), 1) == 0
        )
        for number, guest in enumerate(guest_refs):
            for plane in range(rows):
                density = own_ref[plane] * guest[plane]
                mean = jnp.sum(density, keepdims=True) * (1.0 / points)
                along = product(split(unpack(density - mean, length)), z_table)
                both = product(y_table, split(along))
                base = number * block + plane
                for row in range(rows):
                    piece = both[slabs * row : slabs * (row + 1), :LANES]
                    if row == 0:
                        piece = piece + jnp.where(corner, mean * float(points), 0.0)
                    out[pl.ds(base + rows * row, slabs, stride=pitch), :] = piece
                for row in range(0, rows, 2):
                    even = both[slabs * row : slabs * (row + 1), LANES:]
                    odd = both[slabs * (row + 1) : slabs * (row + 2), LANES:]
                    place = base + rows * (rows + row // 2)
                    out[pl.ds(place, slabs, stride=pitch), :] = jnp.where(lower, even, odd)

    shape = jax.ShapeDtypeStruct((slabs * pitch, LANES), jnp.float32)
    work = call(kernel, shape, weight * count * 12 * length**3 * rows, count * 2**22, [VMEM] * (2 + count))
    return work(own, *guests, entries)


def middle(blocks, pairs, kernel_values, table):
    places, entries, rows, length = table
    slabs = length // rows
    width = kernel_values.shape[1]
    groups = width // LANES
    depth = groups * rows
    tile = 2 * LANES
    lanes = len(pairs) * width

    pitch_in, pitch_out = blocks.shape[0] // slabs, block_pitch(len(pairs) * depth)

    def kernel(in_ref, values, table_ref, out, lines):
        lines[:, rows:, :] = jnp.zeros((slabs, SLOTS - rows, lanes), jnp.float32)
        x_table, back_table = terms(table_ref, places["x"]), terms(table_ref, places["xt"])
        for start in range(0, lanes, tile):
            stop = min(start + tile, lanes)
            for first in range(start, stop, LANES):
                group = first // LANES
                base = pairs[group // groups] * depth + rows * (group % groups)
                for slab in range(slabs):
                    place = slab * pitch_in + base
                    lines[slab, :rows, first : first + LANES] = in_ref[place : place + rows, :]
            line = lines[:, :, start:stop].reshape(slabs * SLOTS, stop - start)
            total = jnp.sum(line, axis=0, keepdims=True)
            spectrum = product(x_table, split(line - total * (1.0 / length)))
            first_row = lax.broadcasted_iota(jnp.int32, spectrum.shape, 0) == 0
            spectrum = spectrum + jnp.where(first_row, total, 0.0)
            scaled = [
                spectrum[:, first - start : first - start + LANES] * values[:, first % width : first % width + LANES]
                for first in range(start, stop, LANES)
            ]
            image = jnp.concatenate(scaled, axis=1)
            solved = product(back_table, split(image)).reshape(slabs, SLOTS, stop - start)
            for first in range(start, stop, LANES):
                for slab in range(slabs):
                    place = slab * pitch_out + rows * (first // LANES)
                    out[place : place + rows, :] = solved[slab, :rows, first - start : first - start + LANES]

    shape = jax.ShapeDtypeStruct((slabs * pitch_out, LANES), jnp.float32)
    scratch = [pltpu.VMEM((slabs, SLOTS, lanes), jnp.float32)]
    work = call(kernel, shape, lanes * 12 * length * length, lanes * 2**12, [VMEM] * 3, scratch)
    return work(blocks, kernel_values, entries)


def potential_plane(block_ref, place, rows, slabs, y_table, z_table, lower):
    pitch = block_ref.shape[0] // slabs

    def across(row):
        return block_ref[pl.ds(place + rows * row, slabs, stride=pitch), :]

    full = jnp.concatenate([across(row) for row in range(rows)], axis=0)
    parts = []
    for row in range(rows // 2):
        shared = across(rows + row)
        parts.append(jnp.where(lower, shared, 0.0))
        parts.append(jnp.where(lower, 0.0, shared))
    wide = jnp.concatenate([full, jnp.concatenate(parts, axis=0)], axis=1)
    along = product(y_table, split(wide))
    return pack(product(split(along), z_table))


def apply_pairs(blocks, own, guests, weights, table):
    places, entries, rows, length = table
    count = len(guests)
    block = rows * rows * length // LANES

    def kernel(weight, block_ref, own_ref, *refs):
        guest_refs, table_ref, total, sent = refs[:count], refs[count], refs[count + 1], refs[count + 2 :]
        lower = lower_lanes()
        y_table, z_table = terms(table_ref, places["yt"]), terms(table_ref, places["zt"])
        for number in range(count):
            for plane in range(rows):
                field = potential_plane(block_ref, number * block + plane, rows, length // rows, y_table, z_table, lower)
                term = (weight[number + 1] * guest_refs[number][plane]) * field
                total[plane] = term if number == 0 else total[plane] + term
                sent[number][plane] = (weight[0] * own_ref[plane]) * field

    shape = packed_shape(rows, length)
    work = call(kernel, [shape] * (1 + count), count * 12 * length**3 * rows, count * 2**22, [SMEM] + [VMEM] * (3 + count))
    return work(weights, blocks, own, *guests, entries)


def add_received(partial, received):
    rows = partial.shape[0]

    def kernel(part, first, second, out):
        for plane in range(rows):
            out[plane] = part[plane] + (first[plane] + second[plane])

    shape = jax.ShapeDtypeStruct(partial.shape, jnp.float32)
    return call(kernel, shape, 2**34, 2**22, [VMEM] * 3)(partial, *received)


def apply_own(blocks, own, others, weights, table):
    places, entries, rows, length = table

    def kernel(weight, block_ref, own_ref, other, table_ref, out):
        lower = lower_lanes()
        y_table, z_table = terms(table_ref, places["yt"]), terms(table_ref, places["zt"])
        for plane in range(rows):
            field = potential_plane(block_ref, plane, rows, length // rows, y_table, z_table, lower)
            out[plane] = -unpack(other[plane] + (weight[0] * own_ref[plane]) * field, length)

    shape = jax.ShapeDtypeStruct((rows, length, length), jnp.float32)
    work = call(kernel, shape, 12 * length**3 * rows, 2**22, [SMEM] + [VMEM] * 4)
    return work(weights, blocks, own, others, entries)


def kernel_lines(length, rows, slab):
    width = rows * length
    shape = (length, width)
    column = lax.broadcasted_iota(jnp.int32, shape, 1)
    group, lane = column // LANES, column % LANES
    shared = group >= rows
    row = jnp.where(shared, 2 * (group - rows) + lane // HALF, group)
    third = jnp.where(shared, LANES + lane % HALF, lane)

    def square(index):
        folded = jnp.minimum(index, length - index)
        return folded * folded

    total = square(lax.broadcasted_iota(jnp.int32, shape, 0)) + square(slab * rows + row) + square(third)
    lowest = (2.0 * math.pi / length) ** 2
    values = 1.0 / (lowest * (1.0 + total.astype(jnp.float32)))
    return jnp.where(total > 0, values, jnp.zeros_like(values)) / float(length**3)


def exchange(blocks):
    slabs = lax.axis_size("space")
    count = blocks.shape[0] // slabs
    group = math.gcd(count, SLOTS)
    cut = blocks.reshape(slabs, count // group, group, LANES)
    return lax.all_to_all(cut, "space", split_axis=0, concat_axis=0, tiled=True).reshape(blocks.shape)


def shards(orbitals, occupations):
    rows, length = orbitals.shape[1:3]
    slabs = lax.axis_size("space")
    groups = lax.axis_size("band")
    band = lax.axis_index("band")
    table = tables(length, slabs, rows) + (rows, length)

    def shifted(array, by):
        return lax.ppermute(array, "band", [(group, (group + by) % groups) for group in range(groups)])

    own = packed_planes(orbitals[0])
    guests = [shifted(own, -1), shifted(own, 2)]
    picks = jnp.stack([band, (band + 1) % groups, (band + groups - 2) % groups])
    weights = occupations.astype(jnp.float32)[picks]
    kernel_values = kernel_lines(length, rows, lax.axis_index("space"))

    own_lines = exchange(forward(own, [own], table))
    pair_blocks = forward(own, guests, table, 16)
    pair_blocks, own_lines = lax.optimization_barrier((pair_blocks, own_lines))
    pair_lines = exchange(pair_blocks)
    own_image = middle(own_lines, [0], kernel_values, table)
    pair_lines, own_image = lax.optimization_barrier((pair_lines, own_image))
    pair_back = exchange(middle(pair_lines, [0, 1], kernel_values, table))
    own_image, pair_back = lax.optimization_barrier((own_image, pair_back))
    own_back = exchange(own_image)
    partial, to_next, to_far = apply_pairs(pair_back, own, guests, weights, table)
    received = [shifted(to_next, 1), shifted(to_far, -2)]
    others = add_received(partial, received)
    return apply_own(own_back, own, others, weights, table)[None]


def solution(mesh):
    placed = (P("band", "space", None, None), P())
    return jax.shard_map(
        shards,
        mesh=mesh,
        in_specs=placed,
        out_specs=P("band", "space", None, None),
        check_vma=False,
    )
```

```python
import math

import jax
import jax.numpy as jnp
import ml_dtypes
import numpy as np
from jax import lax
from jax.experimental import pallas as pl
from jax.experimental.pallas import tpu as pltpu
from jax.sharding import PartitionSpec as P

LANES = 128
HALF = 64
SLOTS = 8
VMEM = pl.BlockSpec(memory_space=pltpu.VMEM)
SMEM = pl.BlockSpec(memory_space=pltpu.SMEM)


def tables(length, slabs, rows):
    index = np.arange(length)
    phase = (index[:, None] * index[None, :]) % length * (2.0 * math.pi / length)
    cas = np.cos(phase) + np.sin(phase)
    wide = np.concatenate([np.arange(LANES), np.arange(LANES, length), np.arange(LANES, length)])
    grouped = np.array([rows * slab + row for row in range(rows) for slab in range(slabs)])
    padded = np.zeros((length, slabs, SLOTS))
    padded[:, :, :rows] = cas.reshape(length, slabs, rows)
    padded = padded.reshape(length, slabs * SLOTS)
    parts = {
        "z": cas[:, wide],
        "y": cas[grouped, :],
        "x": padded,
        "xt": padded.T,
        "yt": cas[:, grouped],
        "zt": cas[wide, :],
    }
    places, pieces, start = {}, [], 0
    for name, part in parts.items():
        height, width = part.shape
        places[name] = (start, height, width)
        start += 2 * height
        high = part.astype(ml_dtypes.bfloat16)
        low = (part - high.astype(np.float64)).astype(ml_dtypes.bfloat16)
        both = np.zeros((2 * height, 2 * LANES), ml_dtypes.bfloat16)
        both[:height, :width], both[height:, :width] = high, low
        pieces.append(both)
    return places, jnp.asarray(np.concatenate(pieces))


def terms(table_ref, place):
    start, height, width = place
    return table_ref[start : start + 2 * height, :width]


def split(value):
    high = value.astype(jnp.bfloat16)
    return high, (value - high.astype(jnp.float32)).astype(jnp.bfloat16)


def dot(left, right):
    return jnp.dot(left, right, preferred_element_type=jnp.float32)


def from_left(table, value):
    height = table.shape[0] // 2
    high, low = split(value)
    both = dot(table, high)
    return both[:height] + (both[height:] + dot(table[:height], low))


def from_right(value, table):
    height, depth = value.shape[0], table.shape[0] // 2
    high, low = split(value)
    both = dot(jnp.concatenate([high, low], axis=0), table[:depth])
    return both[:height] + (both[height:] + dot(high, table[depth:]))


def call(kernel, out_shape, flops, size, in_specs, scratch=()):
    return pl.pallas_call(
        kernel,
        out_shape=out_shape,
        in_specs=in_specs,
        out_specs=jax.tree.map(lambda _: VMEM, out_shape),
        scratch_shapes=list(scratch),
        compiler_params=pltpu.CompilerParams(vmem_limit_bytes=16 * 1024 * 1024),
        cost_estimate=pl.CostEstimate(flops=flops, bytes_accessed=size, transcendentals=0),
    )


def lower_lanes():
    return lax.broadcasted_iota(jnp.int32, (1, LANES), 1) < HALF


def pack(value):
    half = value.shape[0] // 2
    rest = jnp.concatenate([value[:half, LANES:], value[half:, LANES:]], axis=1)
    return jnp.concatenate([value[:, :LANES], rest], axis=0)


def unpack(packed, length):
    rest = packed[length:]
    column = jnp.concatenate([rest[:, :HALF], rest[:, HALF:]], axis=0)
    return jnp.concatenate([packed[:length], column], axis=1)


def packed_shape(rows, length):
    return jax.ShapeDtypeStruct((rows, length * length // LANES, LANES), jnp.float32)


def packed_planes(orbitals):
    rows, length, _ = orbitals.shape

    def kernel(planes, out):
        for plane in range(rows):
            out[plane] = pack(planes[plane])

    return call(kernel, packed_shape(rows, length), 2**18, 2**21, [VMEM])(orbitals)


def block_pitch(depth):
    return depth


def forward(own, guests, table, weight=1):
    places, entries, rows, length = table
    slabs = length // rows
    count = len(guests)
    block = rows * rows * length // LANES
    pitch = block_pitch(count * block)
    points = length * length

    def kernel(*refs):
        own_ref, guest_refs, table_ref, out = refs[0], refs[1 : 1 + count], refs[1 + count], refs[-1]
        z_table, y_table = terms(table_ref, places["z"]), terms(table_ref, places["y"])
        lower = lower_lanes()
        corner = (lax.broadcasted_iota(jnp.int32, (slabs, LANES), 0) == 0) & (
            lax.broadcasted_iota(jnp.int32, (slabs, LANES), 1) == 0
        )
        for number, guest in enumerate(guest_refs):
            for plane in range(rows):
                density = own_ref[plane] * guest[plane]
                mean = jnp.sum(density, keepdims=True) * (1.0 / points)
                both = from_left(y_table, from_right(unpack(density - mean, length), z_table))
                base = number * block + plane
                for row in range(rows):
                    piece = both[slabs * row : slabs * (row + 1), :LANES]
                    if row == 0:
                        piece = piece + jnp.where(corner, mean * float(points), 0.0)
                    out[pl.ds(base + rows * row, slabs, stride=pitch), :] = piece
                for row in range(0, rows, 2):
                    even = both[slabs * row : slabs * (row + 1), LANES:]
                    odd = both[slabs * (row + 1) : slabs * (row + 2), LANES:]
                    place = base + rows * (rows + row // 2)
                    out[pl.ds(place, slabs, stride=pitch), :] = jnp.where(lower, even, odd)

    shape = jax.ShapeDtypeStruct((slabs * pitch, LANES), jnp.float32)
    work = call(kernel, shape, weight * count * 12 * length**3 * rows, count * 2**22, [VMEM] * (2 + count))
    return work(own, *guests, entries)


def middle(blocks, pairs, kernel_values, table):
    places, entries, rows, length = table
    slabs = length // rows
    width = kernel_values.shape[1]
    groups = width // LANES
    depth = groups * rows
    tile = 2 * LANES
    lanes = len(pairs) * width

    pitch_in, pitch_out = blocks.shape[0] // slabs, block_pitch(len(pairs) * depth)

    def kernel(in_ref, values, table_ref, out, lines):
        lines[:, rows:, :] = jnp.zeros((slabs, SLOTS - rows, lanes), jnp.float32)
        x_table, back_table = terms(table_ref, places["x"]), terms(table_ref, places["xt"])
        for start in range(0, lanes, tile):
            stop = min(start + tile, lanes)
            for first in range(start, stop, LANES):
                group = first // LANES
                base = pairs[group // groups] * depth + rows * (group % groups)
                for slab in range(slabs):
                    place = slab * pitch_in + base
                    lines[slab, :rows, first : first + LANES] = in_ref[place : place + rows, :]
            line = lines[:, :, start:stop].reshape(slabs * SLOTS, stop - start)
            total = jnp.sum(line, axis=0, keepdims=True)
            spectrum = from_left(x_table, line - total * (1.0 / length))
            first_row = lax.broadcasted_iota(jnp.int32, spectrum.shape, 0) == 0
            spectrum = spectrum + jnp.where(first_row, total, 0.0)
            scaled = [
                spectrum[:, first - start : first - start + LANES] * values[:, first % width : first % width + LANES]
                for first in range(start, stop, LANES)
            ]
            image = jnp.concatenate(scaled, axis=1)
            solved = from_left(back_table, image).reshape(slabs, SLOTS, stop - start)
            for first in range(start, stop, LANES):
                for slab in range(slabs):
                    place = slab * pitch_out + rows * (first // LANES)
                    out[place : place + rows, :] = solved[slab, :rows, first - start : first - start + LANES]

    shape = jax.ShapeDtypeStruct((slabs * pitch_out, LANES), jnp.float32)
    scratch = [pltpu.VMEM((slabs, SLOTS, lanes), jnp.float32)]
    work = call(kernel, shape, lanes * 12 * length * length, lanes * 2**12, [VMEM] * 3, scratch)
    return work(blocks, kernel_values, entries)


def fields(block_ref, base, rows, slabs, table_ref, places):
    pitch = block_ref.shape[0] // slabs
    lower = lower_lanes()
    y_table, z_table = terms(table_ref, places["yt"]), terms(table_ref, places["zt"])

    def across(row):
        return block_ref[pl.ds(row, slabs, stride=pitch), :]

    planes = []
    for plane in range(rows):
        place = base + plane
        full = jnp.concatenate([across(place + rows * row) for row in range(rows)], axis=0)
        parts = []
        for row in range(rows // 2):
            shared = across(place + rows * (rows + row))
            parts.append(jnp.where(lower, shared, 0.0))
            parts.append(jnp.where(lower, 0.0, shared))
        wide = jnp.concatenate([full, jnp.concatenate(parts, axis=0)], axis=1)
        planes.append(pack(from_right(from_left(y_table, wide), z_table)))
    return planes


def sent_back(blocks, count, own, weights, table):
    places, entries, rows, length = table
    block = rows * rows * length // LANES

    def kernel(weight, block_ref, own_ref, table_ref, *sent):
        for number in range(count):
            made = fields(block_ref, number * block, rows, length // rows, table_ref, places)
            for plane, field in enumerate(made):
                sent[number][plane] = (weight[0] * own_ref[plane]) * field

    shape = packed_shape(rows, length)
    work = call(kernel, [shape] * count, count * 12 * length**3 * rows, count * 2**22, [SMEM] + [VMEM] * 3)
    return work(weights, blocks, own, entries)


def guest_terms(blocks, guests, weights, table):
    places, entries, rows, length = table
    count = len(guests)
    block = rows * rows * length // LANES

    def kernel(weight, block_ref, *refs):
        guest_refs, table_ref, total = refs[:count], refs[count], refs[count + 1]
        for number, guest in enumerate(guest_refs):
            made = fields(block_ref, number * block, rows, length // rows, table_ref, places)
            for plane, field in enumerate(made):
                term = (weight[number + 1] * guest[plane]) * field
                total[plane] = term if number == 0 else total[plane] + term

    shape = packed_shape(rows, length)
    work = call(kernel, shape, count * 12 * length**3 * rows, count * 2**22, [SMEM] + [VMEM] * (2 + count))
    return work(weights, blocks, *guests, entries)


def add_received(partial, received):
    rows = partial.shape[0]

    def kernel(part, first, second, out):
        for plane in range(rows):
            out[plane] = part[plane] + (first[plane] + second[plane])

    shape = jax.ShapeDtypeStruct(partial.shape, jnp.float32)
    return call(kernel, shape, 2**34, 2**22, [VMEM] * 3)(partial, *received)


def apply_own(blocks, own, others, weights, table):
    places, entries, rows, length = table

    def kernel(weight, block_ref, own_ref, other, table_ref, out):
        for plane, field in enumerate(fields(block_ref, 0, rows, length // rows, table_ref, places)):
            out[plane] = -unpack(other[plane] + (weight[0] * own_ref[plane]) * field, length)

    shape = jax.ShapeDtypeStruct((rows, length, length), jnp.float32)
    work = call(kernel, shape, 12 * length**3 * rows, 2**22, [SMEM] + [VMEM] * 4)
    return work(weights, blocks, own, others, entries)


def kernel_lines(length, rows, slab):
    width = rows * length
    shape = (length, width)
    column = lax.broadcasted_iota(jnp.int32, shape, 1)
    group, lane = column // LANES, column % LANES
    shared = group >= rows
    row = jnp.where(shared, 2 * (group - rows) + lane // HALF, group)
    third = jnp.where(shared, LANES + lane % HALF, lane)

    def square(index):
        folded = jnp.minimum(index, length - index)
        return folded * folded

    total = square(lax.broadcasted_iota(jnp.int32, shape, 0)) + square(slab * rows + row) + square(third)
    lowest = (2.0 * math.pi / length) ** 2
    values = 1.0 / (lowest * (1.0 + total.astype(jnp.float32)))
    return jnp.where(total > 0, values, jnp.zeros_like(values)) / float(length**3)


def exchange(blocks):
    slabs = lax.axis_size("space")
    count = blocks.shape[0] // slabs
    group = math.gcd(count, SLOTS)
    cut = blocks.reshape(slabs, count // group, group, LANES)
    return lax.all_to_all(cut, "space", split_axis=0, concat_axis=0, tiled=True).reshape(blocks.shape)


def shards(orbitals, occupations):
    rows, length = orbitals.shape[1:3]
    slabs = lax.axis_size("space")
    groups = lax.axis_size("band")
    band = lax.axis_index("band")
    table = tables(length, slabs, rows) + (rows, length)

    def shifted(array, by):
        return lax.ppermute(array, "band", [(group, (group + by) % groups) for group in range(groups)])

    own = packed_planes(orbitals[0])
    guests = [shifted(own, -1), shifted(own, 2)]
    picks = jnp.stack([band, (band + 1) % groups, (band + groups - 2) % groups])
    weights = occupations.astype(jnp.float32)[picks]
    kernel_values = kernel_lines(length, rows, lax.axis_index("space"))

    own_lines = exchange(forward(own, [own], table))
    pair_blocks = forward(own, guests, table, 16)
    pair_blocks, own_lines = lax.optimization_barrier((pair_blocks, own_lines))
    pair_lines = exchange(pair_blocks)
    own_image = middle(own_lines, [0], kernel_values, table)
    pair_lines, own_image = lax.optimization_barrier((pair_lines, own_image))
    pair_back = exchange(middle(pair_lines, [0, 1], kernel_values, table))
    own_image, pair_back = lax.optimization_barrier((own_image, pair_back))
    own_back = exchange(own_image)
    to_next, to_far = sent_back(pair_back, len(guests), own, weights, table)
    partial = guest_terms(pair_back, guests, weights, table)
    received = [shifted(to_next, 1), shifted(to_far, -2)]
    others = add_received(partial, received)
    return apply_own(own_back, own, others, weights, table)[None]


def solution(mesh):
    placed = (P("band", "space", None, None), P())
    return jax.shard_map(
        shards,
        mesh=mesh,
        in_specs=placed,
        out_specs=P("band", "space", None, None),
        check_vma=False,
    )
```

```python
import math

import jax
import jax.numpy as jnp
import ml_dtypes
import numpy as np
from jax import lax
from jax.experimental import pallas as pl
from jax.experimental.pallas import tpu as pltpu
from jax.sharding import PartitionSpec as P

LANES = 128
HALF = 64
SLOTS = 8
VMEM = pl.BlockSpec(memory_space=pltpu.VMEM)
SMEM = pl.BlockSpec(memory_space=pltpu.SMEM)
ANY = pl.BlockSpec(memory_space=pltpu.HBM)


def tables(length, slabs, rows):
    index = np.arange(length)
    phase = (index[:, None] * index[None, :]) % length * (2.0 * math.pi / length)
    cas = np.cos(phase) + np.sin(phase)
    wide = np.concatenate([np.arange(LANES), np.arange(LANES, length), np.arange(LANES, length)])
    grouped = np.array([rows * slab + row for row in range(rows) for slab in range(slabs)])
    padded = np.zeros((length, slabs, SLOTS))
    padded[:, :, :rows] = cas.reshape(length, slabs, rows)
    padded = padded.reshape(length, slabs * SLOTS)
    parts = {
        "z": cas[:, wide],
        "y": cas[grouped, :],
        "x": padded,
        "xt": padded.T,
        "yt": cas[:, grouped],
        "zt": cas[wide, :],
    }
    places, pieces, start = {}, [], 0
    for name, part in parts.items():
        height, width = part.shape
        places[name] = (start, height, width)
        start += 2 * height
        high = part.astype(ml_dtypes.bfloat16)
        low = (part - high.astype(np.float64)).astype(ml_dtypes.bfloat16)
        both = np.zeros((2 * height, 2 * LANES), ml_dtypes.bfloat16)
        both[:height, :width], both[height:, :width] = high, low
        pieces.append(both)
    return places, jnp.asarray(np.concatenate(pieces))


def terms(table_ref, place):
    start, height, width = place
    return table_ref[start : start + 2 * height, :width]


def split(value):
    high = value.astype(jnp.bfloat16)
    return high, (value - high.astype(jnp.float32)).astype(jnp.bfloat16)


def dot(left, right):
    return jnp.dot(left, right, preferred_element_type=jnp.float32)


def from_left(table, value):
    height = table.shape[0] // 2
    high, low = split(value)
    both = dot(table, high)
    return both[:height] + (both[height:] + dot(table[:height], low))


def from_right(value, table):
    height, depth = value.shape[0], table.shape[0] // 2
    high, low = split(value)
    both = dot(jnp.concatenate([high, low], axis=0), table[:depth])
    return both[:height] + (both[height:] + dot(high, table[depth:]))


def call(kernel, out_shape, flops, size, in_specs, scratch=()):
    return pl.pallas_call(
        kernel,
        out_shape=out_shape,
        in_specs=in_specs,
        out_specs=jax.tree.map(lambda _: VMEM, out_shape),
        scratch_shapes=list(scratch),
        compiler_params=pltpu.CompilerParams(vmem_limit_bytes=16 * 1024 * 1024),
        cost_estimate=pl.CostEstimate(flops=flops, bytes_accessed=size, transcendentals=0),
    )


def lower_lanes():
    return lax.broadcasted_iota(jnp.int32, (1, LANES), 1) < HALF


def pack(value):
    half = value.shape[0] // 2
    rest = jnp.concatenate([value[:half, LANES:], value[half:, LANES:]], axis=1)
    return jnp.concatenate([value[:, :LANES], rest], axis=0)


def unpack(packed, length):
    rest = packed[length:]
    column = jnp.concatenate([rest[:, :HALF], rest[:, HALF:]], axis=0)
    return jnp.concatenate([packed[:length], column], axis=1)


def packed_shape(rows, length):
    return jax.ShapeDtypeStruct((rows, length * length // LANES, LANES), jnp.float32)


def packed_planes(orbitals):
    rows, length, _ = orbitals.shape

    def kernel(planes, out):
        for plane in range(rows):
            out[plane] = pack(planes[plane])

    return call(kernel, packed_shape(rows, length), 2**18, 2**21, [VMEM])(orbitals)


def block_pitch(depth):
    return depth


def forward(own, guests, table, weight=1):
    places, entries, rows, length = table
    slabs = length // rows
    count = len(guests)
    block = rows * rows * length // LANES
    pitch = block_pitch(count * block)
    points = length * length

    def kernel(*refs):
        own_ref, guest_refs, table_ref, out = refs[0], refs[1 : 1 + count], refs[1 + count], refs[-1]
        z_table, y_table = terms(table_ref, places["z"]), terms(table_ref, places["y"])
        lower = lower_lanes()
        corner = (lax.broadcasted_iota(jnp.int32, (slabs, LANES), 0) == 0) & (
            lax.broadcasted_iota(jnp.int32, (slabs, LANES), 1) == 0
        )
        for number, guest in enumerate(guest_refs):
            for plane in range(rows):
                density = own_ref[plane] * guest[plane]
                mean = jnp.sum(density, keepdims=True) * (1.0 / points)
                both = from_left(y_table, from_right(unpack(density - mean, length), z_table))
                base = number * block + plane
                for row in range(rows):
                    piece = both[slabs * row : slabs * (row + 1), :LANES]
                    if row == 0:
                        piece = piece + jnp.where(corner, mean * float(points), 0.0)
                    out[pl.ds(base + rows * row, slabs, stride=pitch), :] = piece
                for row in range(0, rows, 2):
                    even = both[slabs * row : slabs * (row + 1), LANES:]
                    odd = both[slabs * (row + 1) : slabs * (row + 2), LANES:]
                    place = base + rows * (rows + row // 2)
                    out[pl.ds(place, slabs, stride=pitch), :] = jnp.where(lower, even, odd)

    shape = jax.ShapeDtypeStruct((slabs * pitch, LANES), jnp.float32)
    work = call(kernel, shape, weight * count * 12 * length**3 * rows, count * 2**22, [VMEM] * (2 + count))
    return work(own, *guests, entries)


def middle(blocks, pairs, kernel_values, table):
    places, entries, rows, length = table
    slabs = length // rows
    width = kernel_values.shape[1]
    groups = width // LANES
    depth = groups * rows
    tile = 2 * LANES
    lanes = len(pairs) * width

    pitch_in, pitch_out = blocks.shape[0] // slabs, block_pitch(len(pairs) * depth)

    def kernel(source, values, table_ref, out, lines, in_ref, arrived):
        transfer = pltpu.make_async_copy(source, in_ref, arrived)
        transfer.start()
        lines[:, rows:, :] = jnp.zeros((slabs, SLOTS - rows, lanes), jnp.float32)
        x_table, back_table = terms(table_ref, places["x"]), terms(table_ref, places["xt"])
        transfer.wait()
        for start in range(0, lanes, tile):
            stop = min(start + tile, lanes)
            for first in range(start, stop, LANES):
                group = first // LANES
                base = pairs[group // groups] * depth + rows * (group % groups)
                for slab in range(slabs):
                    place = slab * pitch_in + base
                    lines[slab, :rows, first : first + LANES] = in_ref[place : place + rows, :]
            line = lines[:, :, start:stop].reshape(slabs * SLOTS, stop - start)
            total = jnp.sum(line, axis=0, keepdims=True)
            spectrum = from_left(x_table, line - total * (1.0 / length))
            first_row = lax.broadcasted_iota(jnp.int32, spectrum.shape, 0) == 0
            spectrum = spectrum + jnp.where(first_row, total, 0.0)
            scaled = [
                spectrum[:, first - start : first - start + LANES] * values[:, first % width : first % width + LANES]
                for first in range(start, stop, LANES)
            ]
            image = jnp.concatenate(scaled, axis=1)
            solved = from_left(back_table, image).reshape(slabs, SLOTS, stop - start)
            for first in range(start, stop, LANES):
                for slab in range(slabs):
                    place = slab * pitch_out + rows * (first // LANES)
                    out[place : place + rows, :] = solved[slab, :rows, first - start : first - start + LANES]

    shape = jax.ShapeDtypeStruct((slabs * pitch_out, LANES), jnp.float32)
    scratch = [
        pltpu.VMEM((slabs, SLOTS, lanes), jnp.float32),
        pltpu.VMEM(blocks.shape, jnp.float32),
        pltpu.SemaphoreType.DMA(()),
    ]
    work = call(kernel, shape, lanes * 12 * length * length, lanes * 2**12, [ANY, VMEM, VMEM], scratch)
    return work(pltpu.with_memory_space_constraint(blocks, pltpu.HBM), kernel_values, entries)


def fields(block_ref, base, rows, slabs, table_ref, places):
    pitch = block_ref.shape[0] // slabs
    lower = lower_lanes()
    y_table, z_table = terms(table_ref, places["yt"]), terms(table_ref, places["zt"])

    def across(row):
        return block_ref[pl.ds(row, slabs, stride=pitch), :]

    planes = []
    for plane in range(rows):
        place = base + plane
        full = jnp.concatenate([across(place + rows * row) for row in range(rows)], axis=0)
        parts = []
        for row in range(rows // 2):
            shared = across(place + rows * (rows + row))
            parts.append(jnp.where(lower, shared, 0.0))
            parts.append(jnp.where(lower, 0.0, shared))
        wide = jnp.concatenate([full, jnp.concatenate(parts, axis=0)], axis=1)
        planes.append(pack(from_right(from_left(y_table, wide), z_table)))
    return planes


def sent_back(blocks, count, own, weights, table):
    places, entries, rows, length = table
    block = rows * rows * length // LANES

    def kernel(weight, block_ref, own_ref, table_ref, *sent):
        for number in range(count):
            made = fields(block_ref, number * block, rows, length // rows, table_ref, places)
            for plane, field in enumerate(made):
                sent[number][plane] = (weight[0] * own_ref[plane]) * field

    shape = packed_shape(rows, length)
    work = call(kernel, [shape] * count, count * 12 * length**3 * rows, count * 2**22, [SMEM] + [VMEM] * 3)
    return work(weights, blocks, own, entries)


def guest_terms(blocks, guests, weights, table):
    places, entries, rows, length = table
    count = len(guests)
    block = rows * rows * length // LANES

    def kernel(weight, block_ref, *refs):
        guest_refs, table_ref, total = refs[:count], refs[count], refs[count + 1]
        for number, guest in enumerate(guest_refs):
            made = fields(block_ref, number * block, rows, length // rows, table_ref, places)
            for plane, field in enumerate(made):
                term = (weight[number + 1] * guest[plane]) * field
                total[plane] = term if number == 0 else total[plane] + term

    shape = packed_shape(rows, length)
    work = call(kernel, shape, count * 12 * length**3 * rows, count * 2**22, [SMEM] + [VMEM] * (2 + count))
    return work(weights, blocks, *guests, entries)


def add_received(partial, received):
    rows = partial.shape[0]

    def kernel(part, first, second, out):
        for plane in range(rows):
            out[plane] = part[plane] + (first[plane] + second[plane])

    shape = jax.ShapeDtypeStruct(partial.shape, jnp.float32)
    return call(kernel, shape, 2**34, 2**22, [VMEM] * 3)(partial, *received)


def apply_own(blocks, own, others, weights, table):
    places, entries, rows, length = table

    def kernel(weight, block_ref, own_ref, other, table_ref, out, held, arrived):
        transfer = pltpu.make_async_copy(other, held, arrived)
        transfer.start()
        made = fields(block_ref, 0, rows, length // rows, table_ref, places)
        transfer.wait()
        for plane, field in enumerate(made):
            out[plane] = -unpack(held[plane] + (weight[0] * own_ref[plane]) * field, length)

    shape = jax.ShapeDtypeStruct((rows, length, length), jnp.float32)
    scratch = [pltpu.VMEM(others.shape, jnp.float32), pltpu.SemaphoreType.DMA(())]
    work = call(kernel, shape, 12 * length**3 * rows, 2**22, [SMEM, VMEM, VMEM, ANY, VMEM], scratch)
    others = pltpu.with_memory_space_constraint(others, pltpu.HBM)
    return work(weights, blocks, own, others, entries)


def kernel_lines(length, rows, slab):
    width = rows * length
    shape = (length, width)
    column = lax.broadcasted_iota(jnp.int32, shape, 1)
    group, lane = column // LANES, column % LANES
    shared = group >= rows
    row = jnp.where(shared, 2 * (group - rows) + lane // HALF, group)
    third = jnp.where(shared, LANES + lane % HALF, lane)

    def square(index):
        folded = jnp.minimum(index, length - index)
        return folded * folded

    total = square(lax.broadcasted_iota(jnp.int32, shape, 0)) + square(slab * rows + row) + square(third)
    lowest = (2.0 * math.pi / length) ** 2
    values = 1.0 / (lowest * (1.0 + total.astype(jnp.float32)))
    return jnp.where(total > 0, values, jnp.zeros_like(values)) / float(length**3)


def exchange(blocks):
    slabs = lax.axis_size("space")
    count = blocks.shape[0] // slabs
    group = math.gcd(count, SLOTS)
    cut = blocks.reshape(slabs, count // group, group, LANES)
    return lax.all_to_all(cut, "space", split_axis=0, concat_axis=0, tiled=True).reshape(blocks.shape)


def shards(orbitals, occupations):
    rows, length = orbitals.shape[1:3]
    slabs = lax.axis_size("space")
    groups = lax.axis_size("band")
    band = lax.axis_index("band")
    table = tables(length, slabs, rows) + (rows, length)

    def shifted(array, by):
        return lax.ppermute(array, "band", [(group, (group + by) % groups) for group in range(groups)])

    own = packed_planes(orbitals[0])
    guests = [shifted(own, -1), shifted(own, 2)]
    picks = jnp.stack([band, (band + 1) % groups, (band + groups - 2) % groups])
    weights = occupations.astype(jnp.float32)[picks]
    kernel_values = kernel_lines(length, rows, lax.axis_index("space"))

    own_lines = exchange(forward(own, [own], table))
    pair_blocks = forward(own, guests, table, 16)
    pair_blocks, own_lines = lax.optimization_barrier((pair_blocks, own_lines))
    pair_lines = exchange(pair_blocks)
    own_image = middle(own_lines, [0], kernel_values, table)
    pair_lines, own_image = lax.optimization_barrier((pair_lines, own_image))
    pair_back = exchange(middle(pair_lines, [0, 1], kernel_values, table))
    own_image, pair_back = lax.optimization_barrier((own_image, pair_back))
    own_back = exchange(own_image)
    to_next, to_far = sent_back(pair_back, len(guests), own, weights, table)
    partial = guest_terms(pair_back, guests, weights, table)
    received = [shifted(to_next, 1), shifted(to_far, -2)]
    others = add_received(partial, received)
    return apply_own(own_back, own, others, weights, table)[None]


def solution(mesh):
    placed = (P("band", "space", None, None), P())
    return jax.shard_map(
        shards,
        mesh=mesh,
        in_specs=placed,
        out_specs=P("band", "space", None, None),
        check_vma=False,
    )
```

```python
import math

import jax
import jax.numpy as jnp
import ml_dtypes
import numpy as np
from jax import lax
from jax.experimental import pallas as pl
from jax.experimental.pallas import tpu as pltpu
from jax.sharding import PartitionSpec as P

LANES = 128
HALF = 64
SLOTS = 8
VMEM = pl.BlockSpec(memory_space=pltpu.VMEM)
SMEM = pl.BlockSpec(memory_space=pltpu.SMEM)
ANY = pl.BlockSpec(memory_space=pltpu.HBM)


def tables(length, slabs, rows):
    index = np.arange(length)
    phase = (index[:, None] * index[None, :]) % length * (2.0 * math.pi / length)
    cas = np.cos(phase) + np.sin(phase)
    wide = np.concatenate([np.arange(LANES), np.arange(LANES, length), np.arange(LANES, length)])
    grouped = np.array([rows * slab + row for row in range(rows) for slab in range(slabs)])
    padded = np.zeros((length, slabs, SLOTS))
    padded[:, :, :rows] = cas.reshape(length, slabs, rows)
    padded = padded.reshape(length, slabs * SLOTS)
    parts = {
        "z": cas[:, wide],
        "y": cas[grouped, :],
        "x": padded,
        "xt": padded.T,
        "yt": cas[:, grouped],
        "zt": cas[wide, :],
    }
    places, pieces, start = {}, [], 0
    for name, part in parts.items():
        height, width = part.shape
        places[name] = (start, height, width)
        start += 2 * height
        high = part.astype(ml_dtypes.bfloat16)
        low = (part - high.astype(np.float64)).astype(ml_dtypes.bfloat16)
        both = np.zeros((2 * height, 2 * LANES), ml_dtypes.bfloat16)
        both[:height, :width], both[height:, :width] = high, low
        pieces.append(both)
    return places, jnp.asarray(np.concatenate(pieces))


def terms(table_ref, place):
    start, height, width = place
    return table_ref[start : start + 2 * height, :width]


def split(value):
    high = value.astype(jnp.bfloat16)
    return high, (value - high.astype(jnp.float32)).astype(jnp.bfloat16)


def dot(left, right):
    return jnp.dot(left, right, preferred_element_type=jnp.float32)


def from_left(table, value):
    height = table.shape[0] // 2
    high, low = split(value)
    both = dot(table, high)
    return both[:height] + (both[height:] + dot(table[:height], low))


def from_right(value, table):
    height, depth = value.shape[0], table.shape[0] // 2
    high, low = split(value)
    both = dot(jnp.concatenate([high, low], axis=0), table[:depth])
    return both[:height] + (both[height:] + dot(high, table[depth:]))


def call(kernel, out_shape, flops, size, in_specs, scratch=()):
    return pl.pallas_call(
        kernel,
        out_shape=out_shape,
        in_specs=in_specs,
        out_specs=jax.tree.map(lambda _: VMEM, out_shape),
        scratch_shapes=list(scratch),
        compiler_params=pltpu.CompilerParams(vmem_limit_bytes=16 * 1024 * 1024),
        cost_estimate=pl.CostEstimate(flops=flops, bytes_accessed=size, transcendentals=0),
    )


def lower_lanes():
    return lax.broadcasted_iota(jnp.int32, (1, LANES), 1) < HALF


def pack(value):
    half = value.shape[0] // 2
    rest = jnp.concatenate([value[:half, LANES:], value[half:, LANES:]], axis=1)
    return jnp.concatenate([value[:, :LANES], rest], axis=0)


def unpack(packed, length):
    rest = packed[length:]
    column = jnp.concatenate([rest[:, :HALF], rest[:, HALF:]], axis=0)
    return jnp.concatenate([packed[:length], column], axis=1)


def packed_shape(rows, length):
    return jax.ShapeDtypeStruct((rows, length * length // LANES, LANES), jnp.float32)


def packed_planes(orbitals):
    rows, length, _ = orbitals.shape

    def kernel(planes, out):
        for plane in range(rows):
            out[plane] = pack(planes[plane])

    return call(kernel, packed_shape(rows, length), 2**18, 2**21, [VMEM])(orbitals)


def block_pitch(depth):
    return depth


def forward(own, guests, table, weight=1):
    places, entries, rows, length = table
    slabs = length // rows
    count = len(guests)
    block = rows * rows * length // LANES
    pitch = block_pitch(count * block)
    points = length * length

    def kernel(*refs):
        own_ref, guest_refs, table_ref, out = refs[0], refs[1 : 1 + count], refs[1 + count], refs[-1]
        z_table, y_table = terms(table_ref, places["z"]), terms(table_ref, places["y"])
        lower = lower_lanes()
        corner = (lax.broadcasted_iota(jnp.int32, (slabs, LANES), 0) == 0) & (
            lax.broadcasted_iota(jnp.int32, (slabs, LANES), 1) == 0
        )
        for number, guest in enumerate(guest_refs):
            for plane in range(rows):
                density = own_ref[plane] * guest[plane]
                mean = jnp.sum(density, keepdims=True) * (1.0 / points)
                both = from_left(y_table, from_right(unpack(density - mean, length), z_table))
                base = number * block + plane
                for row in range(rows):
                    piece = both[slabs * row : slabs * (row + 1), :LANES]
                    if row == 0:
                        piece = piece + jnp.where(corner, mean * float(points), 0.0)
                    out[pl.ds(base + rows * row, slabs, stride=pitch), :] = piece
                for row in range(0, rows, 2):
                    even = both[slabs * row : slabs * (row + 1), LANES:]
                    odd = both[slabs * (row + 1) : slabs * (row + 2), LANES:]
                    place = base + rows * (rows + row // 2)
                    out[pl.ds(place, slabs, stride=pitch), :] = jnp.where(lower, even, odd)

    shape = jax.ShapeDtypeStruct((slabs * pitch, LANES), jnp.float32)
    work = call(kernel, shape, weight * count * 12 * length**3 * rows, count * 2**22, [VMEM] * (2 + count))
    return work(own, *guests, entries)


def middle(blocks, pairs, kernel_values, table):
    places, entries, rows, length = table
    slabs = length // rows
    width = kernel_values.shape[1]
    groups = width // LANES
    depth = groups * rows
    tile = 2 * LANES
    lanes = len(pairs) * width

    pitch_in, pitch_out = blocks.shape[0] // slabs, block_pitch(len(pairs) * depth)

    def kernel(source, values, table_ref, out, lines, in_ref, arrived):
        transfer = pltpu.make_async_copy(source, in_ref, arrived)
        transfer.start()
        lines[:, rows:, :] = jnp.zeros((slabs, SLOTS - rows, lanes), jnp.float32)
        x_table, back_table = terms(table_ref, places["x"]), terms(table_ref, places["xt"])
        transfer.wait()
        for start in range(0, lanes, tile):
            stop = min(start + tile, lanes)
            for first in range(start, stop, LANES):
                group = first // LANES
                base = pairs[group // groups] * depth + rows * (group % groups)
                for slab in range(slabs):
                    place = slab * pitch_in + base
                    lines[slab, :rows, first : first + LANES] = in_ref[place : place + rows, :]
            line = lines[:, :, start:stop].reshape(slabs * SLOTS, stop - start)
            total = jnp.sum(line, axis=0, keepdims=True)
            spectrum = from_left(x_table, line - total * (1.0 / length))
            first_row = lax.broadcasted_iota(jnp.int32, spectrum.shape, 0) == 0
            spectrum = spectrum + jnp.where(first_row, total, 0.0)
            scaled = [
                spectrum[:, first - start : first - start + LANES] * values[:, first % width : first % width + LANES]
                for first in range(start, stop, LANES)
            ]
            image = jnp.concatenate(scaled, axis=1)
            solved = from_left(back_table, image).reshape(slabs, SLOTS, stop - start)
            for first in range(start, stop, LANES):
                for slab in range(slabs):
                    place = slab * pitch_out + rows * (first // LANES)
                    out[place : place + rows, :] = solved[slab, :rows, first - start : first - start + LANES]

    shape = jax.ShapeDtypeStruct((slabs * pitch_out, LANES), jnp.float32)
    scratch = [
        pltpu.VMEM((slabs, SLOTS, lanes), jnp.float32),
        pltpu.VMEM(blocks.shape, jnp.float32),
        pltpu.SemaphoreType.DMA(()),
    ]
    work = call(kernel, shape, lanes * 12 * length * length, lanes * 2**12, [ANY, VMEM, VMEM], scratch)
    return work(pltpu.with_memory_space_constraint(blocks, pltpu.HBM), kernel_values, entries)


def fields(block_ref, base, rows, slabs, table_ref, places):
    pitch = block_ref.shape[0] // slabs
    lower = lower_lanes()
    y_table, z_table = terms(table_ref, places["yt"]), terms(table_ref, places["zt"])

    def across(row):
        return block_ref[pl.ds(row, slabs, stride=pitch), :]

    planes = []
    for plane in range(rows):
        place = base + plane
        full = jnp.concatenate([across(place + rows * row) for row in range(rows)], axis=0)
        parts = []
        for row in range(rows // 2):
            shared = across(place + rows * (rows + row))
            parts.append(jnp.where(lower, shared, 0.0))
            parts.append(jnp.where(lower, 0.0, shared))
        wide = jnp.concatenate([full, jnp.concatenate(parts, axis=0)], axis=1)
        planes.append(pack(from_right(from_left(y_table, wide), z_table)))
    return planes


def sent_back(blocks, number, own, weights, table):
    places, entries, rows, length = table
    block = rows * rows * length // LANES

    def kernel(weight, block_ref, own_ref, table_ref, sent):
        made = fields(block_ref, number * block, rows, length // rows, table_ref, places)
        for plane, field in enumerate(made):
            sent[plane] = (weight[0] * own_ref[plane]) * field

    work = call(kernel, packed_shape(rows, length), 12 * length**3 * rows, 2**22, [SMEM] + [VMEM] * 3)
    return work(weights, blocks, own, entries)


def guest_terms(blocks, guests, weights, table):
    places, entries, rows, length = table
    count = len(guests)
    block = rows * rows * length // LANES

    def kernel(weight, block_ref, *refs):
        guest_refs, table_ref, total = refs[:count], refs[count], refs[count + 1]
        for number, guest in enumerate(guest_refs):
            made = fields(block_ref, number * block, rows, length // rows, table_ref, places)
            for plane, field in enumerate(made):
                term = (weight[number + 1] * guest[plane]) * field
                total[plane] = term if number == 0 else total[plane] + term

    shape = packed_shape(rows, length)
    work = call(kernel, shape, count * 12 * length**3 * rows, count * 2**22, [SMEM] + [VMEM] * (2 + count))
    return work(weights, blocks, *guests, entries)


def add_received(partial, received):
    rows = partial.shape[0]

    def kernel(part, arrived, out):
        for plane in range(rows):
            out[plane] = part[plane] + arrived[plane]

    shape = jax.ShapeDtypeStruct(partial.shape, jnp.float32)
    return call(kernel, shape, 2**34, 2**22, [VMEM] * 2)(partial, received)


def apply_own(blocks, own, others, weights, table):
    places, entries, rows, length = table

    def kernel(weight, block_ref, own_ref, other, table_ref, out, held, arrived):
        transfer = pltpu.make_async_copy(other, held, arrived)
        transfer.start()
        made = fields(block_ref, 0, rows, length // rows, table_ref, places)
        transfer.wait()
        for plane, field in enumerate(made):
            out[plane] = -unpack(held[plane] + (weight[0] * own_ref[plane]) * field, length)

    shape = jax.ShapeDtypeStruct((rows, length, length), jnp.float32)
    scratch = [pltpu.VMEM(others.shape, jnp.float32), pltpu.SemaphoreType.DMA(())]
    work = call(kernel, shape, 12 * length**3 * rows, 2**22, [SMEM, VMEM, VMEM, ANY, VMEM], scratch)
    others = pltpu.with_memory_space_constraint(others, pltpu.HBM)
    return work(weights, blocks, own, others, entries)


def kernel_lines(length, rows, slab):
    width = rows * length
    shape = (length, width)
    column = lax.broadcasted_iota(jnp.int32, shape, 1)
    group, lane = column // LANES, column % LANES
    shared = group >= rows
    row = jnp.where(shared, 2 * (group - rows) + lane // HALF, group)
    third = jnp.where(shared, LANES + lane % HALF, lane)

    def square(index):
        folded = jnp.minimum(index, length - index)
        return folded * folded

    total = square(lax.broadcasted_iota(jnp.int32, shape, 0)) + square(slab * rows + row) + square(third)
    lowest = (2.0 * math.pi / length) ** 2
    values = 1.0 / (lowest * (1.0 + total.astype(jnp.float32)))
    return jnp.where(total > 0, values, jnp.zeros_like(values)) / float(length**3)


def exchange(blocks):
    slabs = lax.axis_size("space")
    count = blocks.shape[0] // slabs
    group = math.gcd(count, SLOTS)
    cut = blocks.reshape(slabs, count // group, group, LANES)
    return lax.all_to_all(cut, "space", split_axis=0, concat_axis=0, tiled=True).reshape(blocks.shape)


def shards(orbitals, occupations):
    rows, length = orbitals.shape[1:3]
    slabs = lax.axis_size("space")
    groups = lax.axis_size("band")
    band = lax.axis_index("band")
    table = tables(length, slabs, rows) + (rows, length)

    def shifted(array, by):
        return lax.ppermute(array, "band", [(group, (group + by) % groups) for group in range(groups)])

    own = packed_planes(orbitals[0])
    guests = [shifted(own, -1), shifted(own, 2)]
    picks = jnp.stack([band, (band + 1) % groups, (band + groups - 2) % groups])
    weights = occupations.astype(jnp.float32)[picks]
    kernel_values = kernel_lines(length, rows, lax.axis_index("space"))

    own_lines = exchange(forward(own, [own], table))
    pair_blocks = forward(own, guests, table, 16)
    pair_blocks, own_lines = lax.optimization_barrier((pair_blocks, own_lines))
    pair_lines = exchange(pair_blocks)
    own_image = middle(own_lines, [0], kernel_values, table)
    pair_lines, own_image = lax.optimization_barrier((pair_lines, own_image))
    pair_back = exchange(middle(pair_lines, [0, 1], kernel_values, table))
    own_image, pair_back = lax.optimization_barrier((own_image, pair_back))
    own_back = exchange(own_image)
    to_next = sent_back(pair_back, 0, own, weights, table)
    to_far = sent_back(pair_back, 1, own, weights, table)
    partial = guest_terms(pair_back, guests, weights, table)
    from_before, from_far = shifted(to_next, 1), shifted(to_far, -2)
    others = add_received(add_received(partial, from_before), from_far)
    return apply_own(own_back, own, others, weights, table)[None]


def solution(mesh):
    placed = (P("band", "space", None, None), P())
    return jax.shard_map(
        shards,
        mesh=mesh,
        in_specs=placed,
        out_specs=P("band", "space", None, None),
        check_vma=False,
    )
```

```python
import math

import jax
import jax.numpy as jnp
import ml_dtypes
import numpy as np
from jax import lax
from jax.experimental import pallas as pl
from jax.experimental.pallas import tpu as pltpu
from jax.sharding import PartitionSpec as P

LANES = 128
HALF = 64
SLOTS = 8
VMEM = pl.BlockSpec(memory_space=pltpu.VMEM)
SMEM = pl.BlockSpec(memory_space=pltpu.SMEM)
ANY = pl.BlockSpec(memory_space=pltpu.HBM)


def tables(length, slabs, rows):
    index = np.arange(length)
    phase = (index[:, None] * index[None, :]) % length * (2.0 * math.pi / length)
    cas = np.cos(phase) + np.sin(phase)
    wide = np.concatenate([np.arange(LANES), np.arange(LANES, length), np.arange(LANES, length)])
    grouped = np.array([rows * slab + row for row in range(rows) for slab in range(slabs)])
    padded = np.zeros((length, slabs, SLOTS))
    padded[:, :, :rows] = cas.reshape(length, slabs, rows)
    padded = padded.reshape(length, slabs * SLOTS)
    parts = {
        "z": cas[:, wide],
        "y": cas[grouped, :],
        "x": padded,
        "xt": padded.T,
        "yt": cas[:, grouped],
        "zt": cas[wide, :],
    }
    places, pieces, start = {}, [], 0
    for name, part in parts.items():
        height, width = part.shape
        places[name] = (start, height, width)
        start += 2 * height
        high = part.astype(ml_dtypes.bfloat16)
        low = (part - high.astype(np.float64)).astype(ml_dtypes.bfloat16)
        both = np.zeros((2 * height, 2 * LANES), ml_dtypes.bfloat16)
        both[:height, :width], both[height:, :width] = high, low
        pieces.append(both)
    return places, jnp.asarray(np.concatenate(pieces))


def terms(table_ref, place):
    start, height, width = place
    return table_ref[start : start + 2 * height, :width]


def split(value):
    high = value.astype(jnp.bfloat16)
    return high, (value - high.astype(jnp.float32)).astype(jnp.bfloat16)


def dot(left, right):
    return jnp.dot(left, right, preferred_element_type=jnp.float32)


def from_left(table, value):
    height = table.shape[0] // 2
    high, low = split(value)
    both = dot(table, high)
    return both[:height] + (both[height:] + dot(table[:height], low))


def from_right(value, table):
    height, depth = value.shape[0], table.shape[0] // 2
    high, low = split(value)
    both = dot(jnp.concatenate([high, low], axis=0), table[:depth])
    return both[:height] + (both[height:] + dot(high, table[depth:]))


def call(kernel, out_shape, flops, size, in_specs, scratch=()):
    return pl.pallas_call(
        kernel,
        out_shape=out_shape,
        in_specs=in_specs,
        out_specs=jax.tree.map(lambda _: VMEM, out_shape),
        scratch_shapes=list(scratch),
        compiler_params=pltpu.CompilerParams(vmem_limit_bytes=16 * 1024 * 1024),
        cost_estimate=pl.CostEstimate(flops=flops, bytes_accessed=size, transcendentals=0),
    )


def lower_lanes():
    return lax.broadcasted_iota(jnp.int32, (1, LANES), 1) < HALF


def pack(value):
    half = value.shape[0] // 2
    rest = jnp.concatenate([value[:half, LANES:], value[half:, LANES:]], axis=1)
    return jnp.concatenate([value[:, :LANES], rest], axis=0)


def unpack(packed, length):
    rest = packed[length:]
    column = jnp.concatenate([rest[:, :HALF], rest[:, HALF:]], axis=0)
    return jnp.concatenate([packed[:length], column], axis=1)


def packed_shape(rows, length):
    return jax.ShapeDtypeStruct((rows, length * length // LANES, LANES), jnp.float32)


def packed_planes(orbitals):
    rows, length, _ = orbitals.shape

    def kernel(planes, out):
        for plane in range(rows):
            out[plane] = pack(planes[plane])

    return call(kernel, packed_shape(rows, length), 2**18, 2**21, [VMEM])(orbitals)


def block_pitch(depth):
    return depth


def forward(own, guests, table, weight=1):
    places, entries, rows, length = table
    slabs = length // rows
    count = len(guests)
    block = rows * rows * length // LANES
    pitch = block_pitch(count * block)
    points = length * length

    def kernel(*refs):
        own_ref, guest_refs, table_ref, out = refs[0], refs[1 : 1 + count], refs[1 + count], refs[-1]
        z_table, y_table = terms(table_ref, places["z"]), terms(table_ref, places["y"])
        lower = lower_lanes()
        corner = (lax.broadcasted_iota(jnp.int32, (slabs, LANES), 0) == 0) & (
            lax.broadcasted_iota(jnp.int32, (slabs, LANES), 1) == 0
        )
        for number, guest in enumerate(guest_refs):
            for plane in range(rows):
                density = own_ref[plane] * guest[plane]
                mean = jnp.sum(density, keepdims=True) * (1.0 / points)
                both = from_left(y_table, from_right(unpack(density - mean, length), z_table))
                base = number * block + plane
                for row in range(rows):
                    piece = both[slabs * row : slabs * (row + 1), :LANES]
                    if row == 0:
                        piece = piece + jnp.where(corner, mean * float(points), 0.0)
                    out[pl.ds(base + rows * row, slabs, stride=pitch), :] = piece
                for row in range(0, rows, 2):
                    even = both[slabs * row : slabs * (row + 1), LANES:]
                    odd = both[slabs * (row + 1) : slabs * (row + 2), LANES:]
                    place = base + rows * (rows + row // 2)
                    out[pl.ds(place, slabs, stride=pitch), :] = jnp.where(lower, even, odd)

    shape = jax.ShapeDtypeStruct((slabs * pitch, LANES), jnp.float32)
    work = call(kernel, shape, weight * count * 12 * length**3 * rows, count * 2**22, [VMEM] * (2 + count))
    return work(own, *guests, entries)


def middle(blocks, pairs, kernel_values, table):
    places, entries, rows, length = table
    slabs = length // rows
    width = kernel_values.shape[1]
    groups = width // LANES
    depth = groups * rows
    tile = 2 * LANES
    lanes = len(pairs) * width

    pitch_in, pitch_out = blocks.shape[0] // slabs, block_pitch(len(pairs) * depth)

    def kernel(source, values, table_ref, out, lines, in_ref, arrived):
        transfer = pltpu.make_async_copy(source, in_ref, arrived)
        transfer.start()
        lines[:, rows:, :] = jnp.zeros((slabs, SLOTS - rows, lanes), jnp.float32)
        x_table, back_table = terms(table_ref, places["x"]), terms(table_ref, places["xt"])
        transfer.wait()
        for start in range(0, lanes, tile):
            stop = min(start + tile, lanes)
            for first in range(start, stop, LANES):
                group = first // LANES
                base = pairs[group // groups] * depth + rows * (group % groups)
                for slab in range(slabs):
                    place = slab * pitch_in + base
                    lines[slab, :rows, first : first + LANES] = in_ref[place : place + rows, :]
            line = lines[:, :, start:stop].reshape(slabs * SLOTS, stop - start)
            total = jnp.sum(line, axis=0, keepdims=True)
            spectrum = from_left(x_table, line - total * (1.0 / length))
            first_row = lax.broadcasted_iota(jnp.int32, spectrum.shape, 0) == 0
            spectrum = spectrum + jnp.where(first_row, total, 0.0)
            scaled = [
                spectrum[:, first - start : first - start + LANES] * values[:, first % width : first % width + LANES]
                for first in range(start, stop, LANES)
            ]
            image = jnp.concatenate(scaled, axis=1)
            solved = from_left(back_table, image).reshape(slabs, SLOTS, stop - start)
            for first in range(start, stop, LANES):
                for slab in range(slabs):
                    place = slab * pitch_out + rows * (first // LANES)
                    out[place : place + rows, :] = solved[slab, :rows, first - start : first - start + LANES]

    shape = jax.ShapeDtypeStruct((slabs * pitch_out, LANES), jnp.float32)
    scratch = [
        pltpu.VMEM((slabs, SLOTS, lanes), jnp.float32),
        pltpu.VMEM(blocks.shape, jnp.float32),
        pltpu.SemaphoreType.DMA(()),
    ]
    work = call(kernel, shape, lanes * 12 * length * length, lanes * 2**12, [ANY, VMEM, VMEM], scratch)
    return work(pltpu.with_memory_space_constraint(blocks, pltpu.HBM), kernel_values, entries)


def fields(block_ref, base, rows, slabs, table_ref, places):
    pitch = block_ref.shape[0] // slabs
    lower = lower_lanes()
    y_table, z_table = terms(table_ref, places["yt"]), terms(table_ref, places["zt"])

    def across(row):
        return block_ref[pl.ds(row, slabs, stride=pitch), :]

    planes = []
    for plane in range(rows):
        place = base + plane
        full = jnp.concatenate([across(place + rows * row) for row in range(rows)], axis=0)
        parts = []
        for row in range(rows // 2):
            shared = across(place + rows * (rows + row))
            parts.append(jnp.where(lower, shared, 0.0))
            parts.append(jnp.where(lower, 0.0, shared))
        wide = jnp.concatenate([full, jnp.concatenate(parts, axis=0)], axis=1)
        planes.append(pack(from_right(from_left(y_table, wide), z_table)))
    return planes


def sent_back(blocks, number, own, weights, table):
    places, entries, rows, length = table
    block = rows * rows * length // LANES

    def kernel(weight, block_ref, own_ref, table_ref, sent):
        made = fields(block_ref, number * block, rows, length // rows, table_ref, places)
        for plane, field in enumerate(made):
            sent[plane] = (weight[0] * own_ref[plane]) * field

    work = call(kernel, packed_shape(rows, length), 12 * length**3 * rows, 2**22, [SMEM] + [VMEM] * 3)
    return work(weights, blocks, own, entries)


def guest_terms(blocks, guests, weights, table):
    places, entries, rows, length = table
    count = len(guests)
    block = rows * rows * length // LANES

    def kernel(weight, block_ref, *refs):
        guest_refs, table_ref, total = refs[:count], refs[count], refs[count + 1]
        for number, guest in enumerate(guest_refs):
            made = fields(block_ref, number * block, rows, length // rows, table_ref, places)
            for plane, field in enumerate(made):
                term = (weight[number + 1] * guest[plane]) * field
                total[plane] = term if number == 0 else total[plane] + term

    shape = packed_shape(rows, length)
    work = call(kernel, shape, count * 12 * length**3 * rows, count * 2**22, [SMEM] + [VMEM] * (2 + count))
    return work(weights, blocks, *guests, entries)


def add_received(partial, received):
    rows = partial.shape[0]

    def kernel(part, arrived, out):
        for plane in range(rows):
            out[plane] = part[plane] + arrived[plane]

    shape = jax.ShapeDtypeStruct(partial.shape, jnp.float32)
    return call(kernel, shape, 2**34, 2**22, [VMEM] * 2)(partial, received)


def apply_own(blocks, own, others, last, weights, table):
    places, entries, rows, length = table

    def kernel(weight, block_ref, own_ref, other, late, table_ref, out, held, late_held, arrived, late_arrived):
        transfer = pltpu.make_async_copy(other, held, arrived)
        late_transfer = pltpu.make_async_copy(late, late_held, late_arrived)
        transfer.start()
        late_transfer.start()
        made = fields(block_ref, 0, rows, length // rows, table_ref, places)
        transfer.wait()
        late_transfer.wait()
        for plane, field in enumerate(made):
            out[plane] = -unpack(held[plane] + late_held[plane] + (weight[0] * own_ref[plane]) * field, length)

    shape = jax.ShapeDtypeStruct((rows, length, length), jnp.float32)
    scratch = [pltpu.VMEM(others.shape, jnp.float32)] * 2 + [pltpu.SemaphoreType.DMA(())] * 2
    work = call(kernel, shape, 12 * length**3 * rows, 2**22, [SMEM, VMEM, VMEM, ANY, ANY, VMEM], scratch)
    others = pltpu.with_memory_space_constraint(others, pltpu.HBM)
    last = pltpu.with_memory_space_constraint(last, pltpu.HBM)
    return work(weights, blocks, own, others, last, entries)


def kernel_lines(length, rows, slab):
    width = rows * length
    shape = (length, width)
    column = lax.broadcasted_iota(jnp.int32, shape, 1)
    group, lane = column // LANES, column % LANES
    shared = group >= rows
    row = jnp.where(shared, 2 * (group - rows) + lane // HALF, group)
    third = jnp.where(shared, LANES + lane % HALF, lane)

    def square(index):
        folded = jnp.minimum(index, length - index)
        return folded * folded

    total = square(lax.broadcasted_iota(jnp.int32, shape, 0)) + square(slab * rows + row) + square(third)
    lowest = (2.0 * math.pi / length) ** 2
    values = 1.0 / (lowest * (1.0 + total.astype(jnp.float32)))
    return jnp.where(total > 0, values, jnp.zeros_like(values)) / float(length**3)


def exchange(blocks):
    slabs = lax.axis_size("space")
    count = blocks.shape[0] // slabs
    group = math.gcd(count, SLOTS)
    cut = blocks.reshape(slabs, count // group, group, LANES)
    return lax.all_to_all(cut, "space", split_axis=0, concat_axis=0, tiled=True).reshape(blocks.shape)


def shards(orbitals, occupations):
    rows, length = orbitals.shape[1:3]
    slabs = lax.axis_size("space")
    groups = lax.axis_size("band")
    band = lax.axis_index("band")
    table = tables(length, slabs, rows) + (rows, length)

    def shifted(array, by):
        return lax.ppermute(array, "band", [(group, (group + by) % groups) for group in range(groups)])

    own = packed_planes(orbitals[0])
    guests = [shifted(own, -1), shifted(own, 2)]
    picks = jnp.stack([band, (band + 1) % groups, (band + groups - 2) % groups])
    weights = occupations.astype(jnp.float32)[picks]
    kernel_values = kernel_lines(length, rows, lax.axis_index("space"))

    own_lines = exchange(forward(own, [own], table))
    pair_blocks = forward(own, guests, table, 16)
    pair_blocks, own_lines = lax.optimization_barrier((pair_blocks, own_lines))
    pair_lines = exchange(pair_blocks)
    own_image = middle(own_lines, [0], kernel_values, table)
    pair_lines, own_image = lax.optimization_barrier((pair_lines, own_image))
    pair_back = exchange(middle(pair_lines, [0, 1], kernel_values, table))
    own_image, pair_back = lax.optimization_barrier((own_image, pair_back))
    own_back = exchange(own_image)
    to_next = sent_back(pair_back, 0, own, weights, table)
    to_far = sent_back(pair_back, 1, own, weights, table)
    partial = guest_terms(pair_back, guests, weights, table)
    from_before, from_far = shifted(to_next, 1), shifted(to_far, -2)
    others = add_received(partial, from_before)
    return apply_own(own_back, own, others, from_far, weights, table)[None]


def solution(mesh):
    placed = (P("band", "space", None, None), P())
    return jax.shard_map(
        shards,
        mesh=mesh,
        in_specs=placed,
        out_specs=P("band", "space", None, None),
        check_vma=False,
    )
```
